32 devices in a mesh: dom: 8 (over z, y), sub: 4 (over x, core).
Axes of the slice: x: 2, y: 2, z: 4, core: 2. Of those that a mesh axis runs over, the one named last changes fastest.
Arguments:
- fine_latent: bfloat16 [1024, 64, 128], P(('dom', 'sub')), may hold values from -6 to 6
- coarse_latent: bfloat16 [256, 64, 128], P(('dom', 'sub')), may hold values from -6 to 6
- adj_index: int32 [1024, 16], P(('dom', 'sub')), may hold values from 0 to 63
- adj_weight: bfloat16 [1024, 64, 1024], P(('dom', 'sub')), may hold values from -0.1875 to 0.1875
- interp_slot: int32 [1024, 4], P(('dom', 'sub')), may hold values from 0 to 31
- interp_weight: bfloat16 [1024, 64, 256], P(('dom', 'sub')), may hold values from -0.375 to 0.375
- coarse_send: int32 [32, 32, 1], P(('dom', 'sub')), may hold values from 0 to 7
- halo_sub_send: int32 [32, 4, 4], P(('dom', 'sub')), may hold values from 0 to 31
- halo_dom_send: int32 [32, 2, 8], P(('dom', 'sub')), may hold values from 0 to 31
- block_count: int32 [32], P(('dom', 'sub')), may hold values from 16 to 32, as said below
- w_in: bfloat16 [2, 384, 128], replicated, may hold values from -0.3125 to 0.3125
- b_in: float32 [2, 128], replicated, may hold values from -3 to 3
- w_out: bfloat16 [2, 128, 128], replicated, may hold values from -0.5 to 0.5
- ln_gain: float32 [2, 128], replicated, may hold values from 0.25 to 1.75
Outputs:
- fine_out: bfloat16 [1024, 64, 128], P(('dom', 'sub'))
The draws below stay inside these ranges and needn't reach their ends.
Inputs may be any that keep to these rules, and one draw needn't show every extreme that they name: `block_count`: some device has all 32 blocks live and some has half of them.
All inputs are finite; a program needn't handle non-finite values.
Results may differ from the reference program's by a relative error of at most 0.0058.
Values may be sent and summed in bfloat16 or wider, within the bound.
A program may use at most 64 MiB of HBM per device.

```python
import jax
import jax.numpy as jnp
from jax import lax

BLK = 64
LAT = 128
FBLK_DEV = 32
CBLK_DEV = 8
K_A = 16
K_I = 4
SLOTS = 1
HS = 4
HD = 8
STEPS = 2
SHARDS = 32
POOL = 64
FINE_BLKS = 1024
COARSE_BLKS = 256
N_DOM = 8
N_SUB = 4


def draw_block_count(key, part):
    lowest = FBLK_DEV // 2
    counts = jax.random.randint(key, (SHARDS,), lowest, FBLK_DEV + 1)
    order = jax.random.permutation(jax.random.fold_in(key, 7), SHARDS)
    counts = counts.at[order[0]].set(FBLK_DEV).at[order[1]].set(lowest)
    return counts.astype(jnp.int32)


def plant(entries, key, smallest, largest):
    shape = entries.shape
    place = [jax.random.randint(jax.random.fold_in(key, axis), (), 0, shape[axis]) for axis in range(len(shape))]
    entries = entries.at[tuple(place)].set(smallest)
    longest = shape.index(max(shape))
    place[longest] = (place[longest] + 1) % shape[longest]
    return entries.at[tuple(place)].set(largest)


def block_scale(stream_key, shape, cuts, least, high):
    def one(dim, shards_of):
        draws = jax.random.uniform(jax.random.fold_in(jax.random.fold_in(stream_key, 6), dim), (shards_of,), jnp.float32, least / len(cuts), high / len(cuts))
        return jnp.repeat(jnp.exp(draws), shape[dim] // shards_of).reshape((-1,) + (1,) * (len(shape) - dim - 1))

    loudness = one(*cuts[0])
    for cut in cuts[1:]:
        loudness = loudness * one(*cut)
    return loudness


def scatter_about(key, dims, width, bound, pieces=(), kind=jnp.bfloat16):
    drawn = width * jax.random.normal(key, dims, jnp.float32)
    if pieces:
        drawn = drawn * block_scale(key, dims, pieces, -0.22, 0.18)
    return jnp.clip(drawn, -bound, bound).astype(kind)


def setup_inputs(seed: int = 0) -> dict:
    key_of = jax.random.split(jax.random.key(seed), 15)
    fine_latent = scatter_about(key_of[0], (FINE_BLKS, BLK, LAT), 1.0, 6.0, ((0, 32),))
    coarse_latent = scatter_about(key_of[1], (COARSE_BLKS, BLK, LAT), 1.0, 6.0, ((0, 32),))
    adj_index = plant(jax.random.randint(key_of[2], (FINE_BLKS, K_A), 0, POOL), jax.random.fold_in(key_of[2], 1), 0, POOL - 1).astype(jnp.int32)
    adj_weight = scatter_about(key_of[3], (FINE_BLKS, BLK, K_A * BLK), (K_A * BLK) ** -0.5, 0.1875, ((0, 32),))
    interp_slot = plant(jax.random.randint(key_of[4], (FINE_BLKS, K_I), 0, SHARDS * SLOTS), jax.random.fold_in(key_of[4], 1), 0, (SHARDS * SLOTS) - 1).astype(jnp.int32)
    interp_weight = scatter_about(key_of[5], (FINE_BLKS, BLK, K_I * BLK), (K_I * BLK) ** -0.5, 0.375, ((0, 32),))
    coarse_send = plant(jax.random.randint(key_of[6], (SHARDS, SHARDS, SLOTS), 0, CBLK_DEV), jax.random.fold_in(key_of[6], 1), 0, CBLK_DEV - 1).astype(jnp.int32)
    halo_sub_send = plant(jax.random.randint(key_of[7], (SHARDS, N_SUB, HS), 0, FBLK_DEV), jax.random.fold_in(key_of[7], 1), 0, FBLK_DEV - 1).astype(jnp.int32)
    halo_dom_send = plant(jax.random.randint(key_of[8], (SHARDS, 2, HD), 0, FBLK_DEV), jax.random.fold_in(key_of[8], 1), 0, FBLK_DEV - 1).astype(jnp.int32)
    block_count = draw_block_count(jax.random.fold_in(key_of[14], 71), 0)
    w_in = scatter_about(key_of[10], (STEPS, 3 * LAT, LAT), (3 * LAT) ** -0.5, 0.3125)
    b_in = scatter_about(key_of[11], (STEPS, LAT), 0.5, 3.0, (), jnp.float32)
    w_out = scatter_about(key_of[12], (STEPS, LAT, LAT), LAT ** -0.5, 0.5)
    ln_gain = jnp.clip(1.0 + 0.15 * jax.random.normal(key_of[13], (STEPS, LAT), jnp.float32), 0.25, 1.75)
    return dict(fine_latent=fine_latent, coarse_latent=coarse_latent, adj_index=adj_index, adj_weight=adj_weight, interp_slot=interp_slot, interp_weight=interp_weight, coarse_send=coarse_send, halo_sub_send=halo_sub_send, halo_dom_send=halo_dom_send, block_count=block_count, w_in=w_in, b_in=b_in, w_out=w_out, ln_gain=ln_gain)


def layer_norm(values, ln_scale):
    average = lax.optimization_barrier(jnp.mean(values, axis=-1, keepdims=True))
    centred = values - average
    variance = lax.optimization_barrier(jnp.mean(centred * centred, axis=-1, keepdims=True))
    return centred * lax.rsqrt(variance + 1e-05) * ln_scale

def node_update(latent, summed, interp, w_first, b_first, w_second, ln_scale, live_mask):
    joined = jnp.concatenate([latent, summed, interp], axis=-1)
    hidden = jnp.einsum('bic,cl->bil', joined.astype(jnp.float32), w_first.astype(jnp.float32)) + b_first
    hidden = jax.nn.relu(hidden).astype(jnp.bfloat16)
    output = jnp.einsum('bic,cl->bil', hidden.astype(jnp.float32), w_second.astype(jnp.float32))
    updated = latent.astype(jnp.float32) + layer_norm(output, ln_scale)
    return jnp.where(live_mask[:, None, None], updated, jnp.zeros_like(updated)).astype(jnp.bfloat16)

def reference(fine_latent, coarse_latent, adj_index, adj_weight, interp_slot, interp_weight, coarse_send, halo_sub_send, halo_dom_send, block_count, w_in, b_in, w_out, ln_gain):
    fine = fine_latent.reshape(SHARDS, FBLK_DEV, BLK, LAT)
    adj_ids = adj_index.reshape(SHARDS, FBLK_DEV, K_A)
    adj_wts = adj_weight.reshape(SHARDS, FBLK_DEV, BLK, K_A * BLK)
    slot_ids = interp_slot.reshape(SHARDS, FBLK_DEV, K_I)
    interp_wts = interp_weight.reshape(SHARDS, FBLK_DEV, BLK, K_I * BLK)
    sources = jnp.arange(SHARDS, dtype=jnp.int32)
    global_ids = sources[:, None, None] * CBLK_DEV + coarse_send
    slot_table = jnp.transpose(global_ids, (1, 0, 2)).reshape(SHARDS, SHARDS * SLOTS)

    def interp_one(device):
        coarse_ids = slot_table[device][slot_ids[device]]
        coarse_rows = coarse_latent[coarse_ids].reshape(FBLK_DEV, K_I * BLK, LAT)
        mixed = jnp.einsum('bim,bml->bil', interp_wts[device].astype(jnp.float32), coarse_rows.astype(jnp.float32))
        return mixed.astype(jnp.bfloat16)
    interp = lax.map(interp_one, sources)
    live_all = jnp.arange(FBLK_DEV, dtype=jnp.int32)[None, :] < block_count[:, None]
    latent = fine
    for layer_step in range(STEPS):

        def update_one(device, latent=latent, layer_step=layer_step):
            dom_index = device // N_SUB
            sub_index = device % N_SUB
            peer_ids = dom_index * N_SUB + jnp.arange(N_SUB, dtype=jnp.int32)
            sub_blocks = halo_sub_send[peer_ids, sub_index]
            got_sub = latent[peer_ids[:, None], sub_blocks].reshape(N_SUB * HS, BLK, LAT)
            below_id = jnp.maximum(device - N_SUB, 0)
            above_id = jnp.minimum(device + N_SUB, SHARDS - 1)
            from_below = latent[below_id][halo_dom_send[below_id, 0]]
            from_below = jnp.where(dom_index > 0, from_below, jnp.zeros_like(from_below))
            from_above = latent[above_id][halo_dom_send[above_id, 1]]
            from_above = jnp.where(dom_index < N_DOM - 1, from_above, jnp.zeros_like(from_above))
            block_pool = jnp.concatenate([latent[device], got_sub, from_below, from_above], axis=0)
            tile_rows = block_pool[adj_ids[device]].reshape(FBLK_DEV, K_A * BLK, LAT)
            summed = jnp.einsum('bim,bml->bil', adj_wts[device].astype(jnp.float32), tile_rows.astype(jnp.float32)).astype(jnp.bfloat16)
            return node_update(latent[device], summed, interp[device], w_in[layer_step], b_in[layer_step], w_out[layer_step], ln_gain[layer_step], live_all[device])
        latent = lax.map(update_one, sources)
    return latent.reshape(SHARDS * FBLK_DEV, BLK, LAT)
```

```python
import functools
import math

import jax
import jax.numpy as jnp
from jax import lax
from jax.experimental import pallas as pl
from jax.experimental.pallas import tpu as pltpu
from jax.sharding import PartitionSpec as P

MESH = pl.DeviceIdType.MESH


def kernel(
    n_dom,
    n_sub,
    steps,
    adj_index,
    interp_slot,
    coarse_send,
    halo_sub_send,
    halo_dom_send,
    block_count,
    fine_hbm,
    coarse_hbm,
    adj_hbm,
    interp_hbm,
    w_in,
    b_in,
    w_out,
    ln_gain,
    out,
    *scratch,
):
    held = scratch[:steps]
    pools = scratch[steps : 2 * steps]
    sub_outs = scratch[2 * steps : 3 * steps]
    dom_outs = scratch[3 * steps : 4 * steps]
    (
        coarse,
        adj,
        iw,
        coarse_out,
        received,
        interp,
        summed,
        load_sem,
        c_send,
        c_recv,
        s_send,
        s_recv,
        d_send,
        d_recv,
    ) = scratch[4 * steps :]

    n = n_dom * n_sub
    dom, sub = lax.axis_index("dom"), lax.axis_index("sub")
    me = dom * n_sub + sub
    n_fine, rows, lat = out.shape
    slots = coarse_out.shape[1]
    hs = sub_outs[0].shape[1]
    hd = dom_outs[0].shape[1]
    k_a, k_i = adj_index.shape[1], interp_slot.shape[1]

    barrier = pltpu.get_barrier_semaphore()

    def greet(o, _):
        d = lax.rem(me + o, n)
        pl.semaphore_signal(
            barrier, inc=1, device_id=(d // n_sub, lax.rem(d, n_sub)), device_id_type=MESH
        )
        return 0

    lax.fori_loop(1, n, greet, 0)

    loads = [
        pltpu.make_async_copy(src, dst, load_sem.at[i])
        for i, (src, dst) in enumerate(
            [(fine_hbm, held[0]), (coarse_hbm, coarse), (adj_hbm, adj), (interp_hbm, iw)]
        )
    ]
    for copy in loads:
        copy.start()

    def gather_halo(t):
        for i in range(n_sub):
            for s in range(hs):
                sub_outs[t][i, s] = held[t][halo_sub_send[0, i, s]]
        for i in range(2):
            for s in range(hd):
                dom_outs[t][i, s] = held[t][halo_dom_send[0, i, s]]

    def sub_copy(t, peer, owner):
        return pltpu.make_async_remote_copy(
            src_ref=sub_outs[t].at[peer],
            dst_ref=pools[t].at[pl.ds(n_fine + owner * hs, hs)],
            send_sem=s_send.at[t, peer],
            recv_sem=s_recv.at[t, owner],
            device_id=(dom, peer),
            device_id_type=MESH,
        )

    def dom_copy(t, way):
        target = dom + 1 if way == 0 else dom - 1
        return pltpu.make_async_remote_copy(
            src_ref=dom_outs[t].at[way],
            dst_ref=pools[t].at[pl.ds(n_fine + n_sub * hs + way * hd, hd)],
            send_sem=d_send.at[t, way],
            recv_sem=d_recv.at[t, way],
            device_id=(target, sub),
            device_id_type=MESH,
        )

    def coarse_copy(peer, owner):
        return pltpu.make_async_remote_copy(
            src_ref=coarse_out.at[peer],
            dst_ref=received.at[pl.ds(owner * slots, slots)],
            send_sem=c_send.at[peer],
            recv_sem=c_recv.at[owner],
            device_id=(peer // n_sub, lax.rem(peer, n_sub)),
            device_id_type=MESH,
        )

    def start_halo(t):
        @pl.when(dom < n_dom - 1)
        def _():
            dom_copy(t, 0).start()

        @pl.when(dom > 0)
        def _():
            dom_copy(t, 1).start()

        for o in range(1, n_sub):
            sub_copy(t, lax.rem(sub + o, n_sub), sub).start()

    def local_pool(t):
        pools[t][pl.ds(n_fine + sub * hs, hs)] = sub_outs[t][sub]
        base = n_fine + n_sub * hs

        @pl.when(dom == 0)
        def _():
            pools[t][pl.ds(base, hd)] = jnp.zeros((hd, rows, lat), pools[t].dtype)

        @pl.when(dom == n_dom - 1)
        def _():
            pools[t][pl.ds(base + hd, hd)] = jnp.zeros((hd, rows, lat), pools[t].dtype)

    def wait_halo(t):
        for o in range(1, n_sub):
            owner = lax.rem(sub + o, n_sub)
            sub_copy(t, owner, owner).wait_recv()

        @pl.when(dom > 0)
        def _():
            dom_copy(t, 0).wait_recv()

        @pl.when(dom < n_dom - 1)
        def _():
            dom_copy(t, 1).wait_recv()

    def finish_halo_sends(t):
        for o in range(1, n_sub):
            sub_copy(t, lax.rem(sub + o, n_sub), sub).wait_send()

        @pl.when(dom < n_dom - 1)
        def _():
            dom_copy(t, 0).wait_send()

        @pl.when(dom > 0)
        def _():
            dom_copy(t, 1).wait_send()

    loads[0].wait()
    gather_halo(0)
    loads[1].wait()

    def gather_coarse(d, _):
        for s in range(slots):
            coarse_out[d, s] = coarse[coarse_send[0, d, s]]
        return 0

    lax.fori_loop(0, n, gather_coarse, 0)

    pl.semaphore_wait(barrier, n - 1)
    start_halo(0)

    def send_coarse(o, _):
        coarse_copy(lax.rem(me + o, n), me).start()
        return 0

    lax.fori_loop(1, n, send_coarse, 0)

    received[pl.ds(me * slots, slots)] = coarse_out[me]
    pools[0][pl.ds(0, n_fine)] = held[0][...]
    local_pool(0)

    group = math.gcd(n_fine, 4)

    def product(weights, table, index, tiles, into):
        def body(g, _):
            for u in range(group):
                b = g * group + u
                picked = jnp.concatenate([table[index[b, k]] for k in range(tiles)], axis=0)
                into[b] = jnp.dot(
                    weights[b], picked, preferred_element_type=jnp.float32
                ).astype(into.dtype)
            return 0

        lax.fori_loop(0, n_fine // group, body, 0)

    chunk = math.gcd(n_fine, 8)
    live = block_count[0]

    for t in range(steps):
        wait_halo(t)
        if t == 0:
            loads[2].wait()
        product(adj, pools[t], adj_index, k_a, summed)
        if t == 0:
            def take_coarse(o, _):
                owner = lax.rem(me + n - o, n)
                coarse_copy(owner, owner).wait_recv()
                return 0

            lax.fori_loop(1, n, take_coarse, 0)
            loads[3].wait()
            product(iw, received, interp_slot, k_i, interp)

        def update(c, _):
            at = pl.ds(c * chunk, chunk)
            h = held[t][at].reshape(chunk * rows, lat)
            joined = jnp.concatenate(
                [
                    h,
                    summed[at].reshape(chunk * rows, lat),
                    interp[at].reshape(chunk * rows, lat),
                ],
                axis=1,
            )
            hidden = jnp.dot(joined, w_in[t], preferred_element_type=jnp.float32)
            hidden = jnp.maximum(hidden + b_in[pl.ds(t, 1)], 0.0).astype(jnp.bfloat16)
            value = jnp.dot(hidden, w_out[t], preferred_element_type=jnp.float32)
            centred = value - jnp.mean(value, axis=-1, keepdims=True)
            variance = jnp.mean(centred * centred, axis=-1, keepdims=True)
            normed = centred * lax.rsqrt(variance + 1e-05) * ln_gain[pl.ds(t, 1)]
            updated = (h.astype(jnp.float32) + normed).reshape(chunk, rows, lat)
            block = c * chunk + lax.broadcasted_iota(jnp.int32, (chunk, rows, lat), 0)
            updated = jnp.where(block < live, updated, 0.0).astype(out.dtype)
            if t == steps - 1:
                out[at] = updated
            else:
                held[t + 1][at] = updated
                pools[t + 1][at] = updated
            return 0

        lax.fori_loop(0, n_fine // chunk, update, 0)
        if t < steps - 1:
            gather_halo(t + 1)
            start_halo(t + 1)
            local_pool(t + 1)

    for t in range(steps):
        finish_halo_sends(t)

    def sent_coarse(o, _):
        coarse_copy(lax.rem(me + o, n), me).wait_send()
        return 0

    lax.fori_loop(1, n, sent_coarse, 0)


def per_device(
    n_dom,
    n_sub,
    fine_latent,
    coarse_latent,
    adj_index,
    adj_weight,
    interp_slot,
    interp_weight,
    coarse_send,
    halo_sub_send,
    halo_dom_send,
    block_count,
    w_in,
    b_in,
    w_out,
    ln_gain,
):
    n = n_dom * n_sub
    steps = w_in.shape[0]
    n_fine, rows, lat = fine_latent.shape
    slots = coarse_send.shape[2]
    hs, hd = halo_sub_send.shape[2], halo_dom_send.shape[2]
    pool = n_fine + n_sub * hs + 2 * hd
    kind = fine_latent.dtype

    def vmem(*lead):
        return pltpu.VMEM(lead + (rows, lat), kind)

    dma = pltpu.SemaphoreType.DMA
    scratch = (
        [vmem(n_fine)] * steps
        + [vmem(pool)] * steps
        + [vmem(n_sub, hs)] * steps
        + [vmem(2, hd)] * steps
        + [
            pltpu.VMEM(coarse_latent.shape, kind),
            pltpu.VMEM(adj_weight.shape, kind),
            pltpu.VMEM(interp_weight.shape, kind),
            vmem(n, slots),
            vmem(n * slots),
            vmem(n_fine),
            vmem(n_fine),
            dma((4,)),
            dma((n,)),
            dma((n,)),
            dma((steps, n_sub)),
            dma((steps, n_sub)),
            dma((steps, 2)),
            dma((steps, 2)),
        ]
    )
    smem = pl.BlockSpec(memory_space=pltpu.SMEM)
    hbm = pl.BlockSpec(memory_space=pl.ANY)
    whole = pl.BlockSpec(memory_space=pltpu.VMEM)
    return pl.pallas_call(
        functools.partial(kernel, n_dom, n_sub, steps),
        out_shape=jax.ShapeDtypeStruct(fine_latent.shape, kind),
        in_specs=[smem] * 6 + [hbm] * 4 + [whole] * 4,
        out_specs=whole,
        scratch_shapes=scratch,
        compiler_params=pltpu.CompilerParams(
            collective_id=0, has_side_effects=True, vmem_limit_bytes=48 * 1024 * 1024
        ),
        name="graph_steps",
    )(
        adj_index,
        interp_slot,
        coarse_send,
        halo_sub_send,
        halo_dom_send,
        block_count,
        fine_latent,
        coarse_latent,
        adj_weight,
        interp_weight,
        w_in,
        b_in,
        w_out,
        ln_gain,
    )


def solution(mesh):
    placed = (
        P(("dom", "sub"), None, None),
        P(("dom", "sub"), None, None),
        P(("dom", "sub"), None),
        P(("dom", "sub"), None, None),
        P(("dom", "sub"), None),
        P(("dom", "sub"), None, None),
        P(("dom", "sub"), None, None),
        P(("dom", "sub"), None, None),
        P(("dom", "sub"), None, None),
        P(("dom", "sub")),
        P(),
        P(),
        P(),
        P(),
    )
    return jax.shard_map(
        functools.partial(per_device, mesh.shape["dom"], mesh.shape["sub"]),
        mesh=mesh,
        in_specs=placed,
        out_specs=P(("dom", "sub"), None, None),
        check_vma=False,
    )
```

```python
import functools
import math

import jax
import jax.numpy as jnp
from jax import lax
from jax.experimental import pallas as pl
from jax.experimental.pallas import tpu as pltpu
from jax.sharding import PartitionSpec as P

MESH = pl.DeviceIdType.MESH


def kernel(
    n_dom,
    n_sub,
    steps,
    adj_index,
    interp_slot,
    coarse_send,
    halo_sub_send,
    halo_dom_send,
    block_count,
    fine_hbm,
    coarse_hbm,
    adj_hbm,
    interp_hbm,
    w_in,
    b_in,
    w_out,
    ln_gain,
    out,
    *scratch,
):
    held = scratch[:steps]
    pools = scratch[steps : 2 * steps]
    sub_outs = scratch[2 * steps : 3 * steps]
    dom_outs = scratch[3 * steps : 4 * steps]
    (
        coarse,
        adj,
        iw,
        coarse_out,
        received,
        interp,
        summed,
        load_sem,
        c_send,
        c_recv,
        s_send,
        s_recv,
        d_send,
        d_recv,
    ) = scratch[4 * steps :]

    n = n_dom * n_sub
    dom, sub = lax.axis_index("dom"), lax.axis_index("sub")
    me = dom * n_sub + sub
    n_fine, rows, lat = out.shape
    slots = coarse_out.shape[1]
    hs = sub_outs[0].shape[1]
    hd = dom_outs[0].shape[1]
    k_a, k_i = adj_index.shape[0], interp_slot.shape[0]

    barrier = pltpu.get_barrier_semaphore()

    def greet(o, _):
        d = lax.rem(me + o, n)
        pl.semaphore_signal(
            barrier, inc=1, device_id=(d // n_sub, lax.rem(d, n_sub)), device_id_type=MESH
        )
        return 0

    lax.fori_loop(1, n, greet, 0)

    loads = [
        pltpu.make_async_copy(src, dst, load_sem.at[i])
        for i, (src, dst) in enumerate(
            [(fine_hbm, held[0]), (coarse_hbm, coarse), (adj_hbm, adj), (interp_hbm, iw)]
        )
    ]
    for copy in loads:
        copy.start()

    def gather_halo(t):
        for i in range(n_sub):
            for s in range(hs):
                sub_outs[t][i, s] = held[t][halo_sub_send[0, i, s]]
        for i in range(2):
            for s in range(hd):
                dom_outs[t][i, s] = held[t][halo_dom_send[0, i, s]]

    def sub_copy(t, peer, owner):
        return pltpu.make_async_remote_copy(
            src_ref=sub_outs[t].at[peer],
            dst_ref=pools[t].at[pl.ds(n_fine + owner * hs, hs)],
            send_sem=s_send.at[t, peer],
            recv_sem=s_recv.at[t, owner],
            device_id=(dom, peer),
            device_id_type=MESH,
        )

    def dom_copy(t, way):
        target = dom + 1 if way == 0 else dom - 1
        return pltpu.make_async_remote_copy(
            src_ref=dom_outs[t].at[way],
            dst_ref=pools[t].at[pl.ds(n_fine + n_sub * hs + way * hd, hd)],
            send_sem=d_send.at[t, way],
            recv_sem=d_recv.at[t, way],
            device_id=(target, sub),
            device_id_type=MESH,
        )

    def coarse_copy(peer, owner):
        return pltpu.make_async_remote_copy(
            src_ref=coarse_out.at[peer],
            dst_ref=received.at[pl.ds(owner * slots, slots)],
            send_sem=c_send.at[peer],
            recv_sem=c_recv.at[owner],
            device_id=(peer // n_sub, lax.rem(peer, n_sub)),
            device_id_type=MESH,
        )

    def start_halo(t):
        @pl.when(dom < n_dom - 1)
        def _():
            dom_copy(t, 0).start()

        @pl.when(dom > 0)
        def _():
            dom_copy(t, 1).start()

        for o in range(1, n_sub):
            sub_copy(t, lax.rem(sub + o, n_sub), sub).start()

    def local_pool(t):
        pools[t][pl.ds(n_fine + sub * hs, hs)] = sub_outs[t][sub]
        base = n_fine + n_sub * hs

        @pl.when(dom == 0)
        def _():
            pools[t][pl.ds(base, hd)] = jnp.zeros((hd, rows, lat), pools[t].dtype)

        @pl.when(dom == n_dom - 1)
        def _():
            pools[t][pl.ds(base + hd, hd)] = jnp.zeros((hd, rows, lat), pools[t].dtype)

    def wait_halo(t):
        for o in range(1, n_sub):
            owner = lax.rem(sub + o, n_sub)
            sub_copy(t, owner, owner).wait_recv()

        @pl.when(dom > 0)
        def _():
            dom_copy(t, 0).wait_recv()

        @pl.when(dom < n_dom - 1)
        def _():
            dom_copy(t, 1).wait_recv()

    def finish_halo_sends(t):
        for o in range(1, n_sub):
            sub_copy(t, lax.rem(sub + o, n_sub), sub).wait_send()

        @pl.when(dom < n_dom - 1)
        def _():
            dom_copy(t, 0).wait_send()

        @pl.when(dom > 0)
        def _():
            dom_copy(t, 1).wait_send()

    loads[0].wait()
    gather_halo(0)
    loads[1].wait()

    def gather_coarse(d, _):
        for s in range(slots):
            coarse_out[d, s] = coarse[coarse_send[0, s, d]]
        return 0

    lax.fori_loop(0, n, gather_coarse, 0)

    pl.semaphore_wait(barrier, n - 1)
    start_halo(0)

    def send_coarse(o, _):
        coarse_copy(lax.rem(me + o, n), me).start()
        return 0

    lax.fori_loop(1, n, send_coarse, 0)

    received[pl.ds(me * slots, slots)] = coarse_out[me]
    pools[0][pl.ds(0, n_fine)] = held[0][...]
    local_pool(0)

    group = math.gcd(n_fine, 4)

    def product(weights, table, index, tiles, into):
        def body(g, _):
            for u in range(group):
                b = g * group + u
                picked = jnp.concatenate([table[index[k, b]] for k in range(tiles)], axis=0)
                into[b] = jnp.dot(
                    weights[b], picked, preferred_element_type=jnp.float32
                ).astype(into.dtype)
            return 0

        lax.fori_loop(0, n_fine // group, body, 0)

    chunk = math.gcd(n_fine, 8)
    live = block_count[0, 0]

    for t in range(steps):
        wait_halo(t)
        if t == 0:
            loads[2].wait()
        product(adj, pools[t], adj_index, k_a, summed)
        if t == 0:
            def take_coarse(o, _):
                owner = lax.rem(me + n - o, n)
                coarse_copy(owner, owner).wait_recv()
                return 0

            lax.fori_loop(1, n, take_coarse, 0)
            loads[3].wait()
            product(iw, received, interp_slot, k_i, interp)

        def update(c, _):
            at = pl.ds(c * chunk, chunk)
            h = held[t][at].reshape(chunk * rows, lat)
            joined = jnp.concatenate(
                [
                    h,
                    summed[at].reshape(chunk * rows, lat),
                    interp[at].reshape(chunk * rows, lat),
                ],
                axis=1,
            )
            hidden = jnp.dot(joined, w_in[t], preferred_element_type=jnp.float32)
            hidden = jnp.maximum(hidden + b_in[pl.ds(t, 1)], 0.0).astype(jnp.bfloat16)
            value = jnp.dot(hidden, w_out[t], preferred_element_type=jnp.float32)
            centred = value - jnp.mean(value, axis=-1, keepdims=True)
            variance = jnp.mean(centred * centred, axis=-1, keepdims=True)
            normed = centred * lax.rsqrt(variance + 1e-05) * ln_gain[pl.ds(t, 1)]
            updated = (h.astype(jnp.float32) + normed).reshape(chunk, rows, lat)
            block = c * chunk + lax.broadcasted_iota(jnp.int32, (chunk, rows, lat), 0)
            updated = jnp.where(block < live, updated, 0.0).astype(out.dtype)
            if t == steps - 1:
                out[at] = updated
            else:
                held[t + 1][at] = updated
                pools[t + 1][at] = updated
            return 0

        lax.fori_loop(0, n_fine // chunk, update, 0)
        if t < steps - 1:
            gather_halo(t + 1)
            start_halo(t + 1)
            local_pool(t + 1)

    for t in range(steps):
        finish_halo_sends(t)

    def sent_coarse(o, _):
        coarse_copy(lax.rem(me + o, n), me).wait_send()
        return 0

    lax.fori_loop(1, n, sent_coarse, 0)


def per_device(
    n_dom,
    n_sub,
    fine_latent,
    coarse_latent,
    adj_index,
    adj_weight,
    interp_slot,
    interp_weight,
    coarse_send,
    halo_sub_send,
    halo_dom_send,
    block_count,
    w_in,
    b_in,
    w_out,
    ln_gain,
):
    n = n_dom * n_sub
    steps = w_in.shape[0]
    n_fine, rows, lat = fine_latent.shape
    slots = coarse_send.shape[2]
    hs, hd = halo_sub_send.shape[2], halo_dom_send.shape[2]
    pool = n_fine + n_sub * hs + 2 * hd
    kind = fine_latent.dtype

    def vmem(*lead):
        return pltpu.VMEM(lead + (rows, lat), kind)

    dma = pltpu.SemaphoreType.DMA
    scratch = (
        [vmem(n_fine)] * steps
        + [vmem(pool)] * steps
        + [vmem(n_sub, hs)] * steps
        + [vmem(2, hd)] * steps
        + [
            pltpu.VMEM(coarse_latent.shape, kind),
            pltpu.VMEM(adj_weight.shape, kind),
            pltpu.VMEM(interp_weight.shape, kind),
            vmem(n, slots),
            vmem(n * slots),
            vmem(n_fine),
            vmem(n_fine),
            dma((4,)),
            dma((n,)),
            dma((n,)),
            dma((steps, n_sub)),
            dma((steps, n_sub)),
            dma((steps, 2)),
            dma((steps, 2)),
        ]
    )
    smem = pl.BlockSpec(memory_space=pltpu.SMEM)
    hbm = pl.BlockSpec(memory_space=pl.ANY)
    whole = pl.BlockSpec(memory_space=pltpu.VMEM)
    return pl.pallas_call(
        functools.partial(kernel, n_dom, n_sub, steps),
        out_shape=jax.ShapeDtypeStruct(fine_latent.shape, kind),
        in_specs=[smem] * 6 + [hbm] * 4 + [whole] * 4,
        out_specs=whole,
        scratch_shapes=scratch,
        compiler_params=pltpu.CompilerParams(
            collective_id=0, has_side_effects=True, vmem_limit_bytes=67043328
        ),
        name="graph_steps",
    )(
        adj_index.T,
        interp_slot.T,
        coarse_send.transpose(0, 2, 1),
        halo_sub_send,
        halo_dom_send,
        block_count.reshape(1, 1),
        fine_latent,
        coarse_latent,
        adj_weight,
        interp_weight,
        w_in,
        b_in,
        w_out,
        ln_gain,
    )


def solution(mesh):
    placed = (
        P(("dom", "sub"), None, None),
        P(("dom", "sub"), None, None),
        P(("dom", "sub"), None),
        P(("dom", "sub"), None, None),
        P(("dom", "sub"), None),
        P(("dom", "sub"), None, None),
        P(("dom", "sub"), None, None),
        P(("dom", "sub"), None, None),
        P(("dom", "sub"), None, None),
        P(("dom", "sub")),
        P(),
        P(),
        P(),
        P(),
    )
    return jax.shard_map(
        functools.partial(per_device, mesh.shape["dom"], mesh.shape["sub"]),
        mesh=mesh,
        in_specs=placed,
        out_specs=P(("dom", "sub"), None, None),
        check_vma=False,
    )
```

```python
import functools
import math

import jax
import jax.numpy as jnp
from jax import lax
from jax.experimental import pallas as pl
from jax.experimental.pallas import tpu as pltpu
from jax.sharding import PartitionSpec as P

MESH = pl.DeviceIdType.MESH


def kernel(
    n_dom,
    n_sub,
    steps,
    adj_index,
    interp_slot,
    coarse_send,
    halo_sub_send,
    halo_dom_send,
    block_count,
    fine_hbm,
    coarse_hbm,
    adj_hbm,
    interp_hbm,
    w_in_hbm,
    b_in_hbm,
    w_out_hbm,
    ln_gain_hbm,
    out_hbm,
    *scratch,
):
    held = scratch[:steps]
    pools = scratch[steps : 2 * steps]
    sub_outs = scratch[2 * steps : 3 * steps]
    dom_outs = scratch[3 * steps : 4 * steps]
    (
        coarse,
        adj,
        iw,
        coarse_out,
        received,
        interp,
        summed,
        w_in,
        b_in,
        w_out,
        ln_gain,
        load_sem,
        out,
        out_sem,
        c_send,
        c_recv,
        s_send,
        s_recv,
        d_send,
        d_recv,
    ) = scratch[4 * steps :]

    n = n_dom * n_sub
    dom, sub = lax.axis_index("dom"), lax.axis_index("sub")
    me = dom * n_sub + sub
    n_fine, rows, lat = out_hbm.shape
    slots = coarse_out.shape[1]
    hs = sub_outs[0].shape[1]
    hd = dom_outs[0].shape[1]
    k_a, k_i = adj_index.shape[0], interp_slot.shape[0]

    barrier = pltpu.get_barrier_semaphore()

    def wrapped(position, size):
        return jnp.where(position >= size, position - size, position)

    subs = [wrapped(sub + o, n_sub) for o in range(n_sub)]
    ways = sorted(range(1, n_dom), key=lambda o: abs(o - n_dom // 2))

    def peers(act):
        for o in ways + [0]:
            to = wrapped(dom + o, n_dom)
            for other in subs[1:] if o == 0 else subs:
                act(to, other)

    def greet(to, other):
        pl.semaphore_signal(barrier, inc=1, device_id=(to, other), device_id_type=MESH)

    peers(greet)

    loads = [
        pltpu.make_async_copy(src, dst, load_sem.at[i])
        for i, (src, dst) in enumerate(
            [
                (fine_hbm, held[0]),
                (coarse_hbm, coarse),
                (adj_hbm, adj),
                (interp_hbm, iw),
                (w_in_hbm, w_in),
                (b_in_hbm, b_in),
                (w_out_hbm, w_out),
                (ln_gain_hbm, ln_gain),
            ]
        )
    ]
    for copy in loads:
        copy.start()

    def gather_halo(t):
        for i in range(n_sub):
            for s in range(hs):
                sub_outs[t][i, s] = held[t][halo_sub_send[0, i, s]]
        for i in range(2):
            for s in range(hd):
                dom_outs[t][i, s] = held[t][halo_dom_send[0, i, s]]

    def sub_copy(t, peer, owner):
        return pltpu.make_async_remote_copy(
            src_ref=sub_outs[t].at[peer],
            dst_ref=pools[t].at[pl.ds(n_fine + owner * hs, hs)],
            send_sem=s_send.at[t, peer],
            recv_sem=s_recv.at[t, owner],
            device_id=(dom, peer),
            device_id_type=MESH,
        )

    def dom_copy(t, way):
        target = dom + 1 if way == 0 else dom - 1
        return pltpu.make_async_remote_copy(
            src_ref=dom_outs[t].at[way],
            dst_ref=pools[t].at[pl.ds(n_fine + n_sub * hs + way * hd, hd)],
            send_sem=d_send.at[t, way],
            recv_sem=d_recv.at[t, way],
            device_id=(target, sub),
            device_id_type=MESH,
        )

    def coarse_copy(to, other, owner):
        peer = to * n_sub + other
        return pltpu.make_async_remote_copy(
            src_ref=coarse_out.at[peer],
            dst_ref=received.at[pl.ds(owner * slots, slots)],
            send_sem=c_send.at[peer],
            recv_sem=c_recv.at[owner],
            device_id=(to, other),
            device_id_type=MESH,
        )

    def start_halo(t):
        @pl.when(dom < n_dom - 1)
        def _():
            dom_copy(t, 0).start()

        @pl.when(dom > 0)
        def _():
            dom_copy(t, 1).start()

        for o in range(1, n_sub):
            sub_copy(t, subs[o], sub).start()

    def local_pool(t):
        pools[t][pl.ds(n_fine + sub * hs, hs)] = sub_outs[t][sub]
        base = n_fine + n_sub * hs

        @pl.when(dom == 0)
        def _():
            pools[t][pl.ds(base, hd)] = jnp.zeros((hd, rows, lat), pools[t].dtype)

        @pl.when(dom == n_dom - 1)
        def _():
            pools[t][pl.ds(base + hd, hd)] = jnp.zeros((hd, rows, lat), pools[t].dtype)

    def wait_halo(t):
        for o in range(1, n_sub):
            owner = subs[o]
            sub_copy(t, owner, owner).wait_recv()

        @pl.when(dom > 0)
        def _():
            dom_copy(t, 0).wait_recv()

        @pl.when(dom < n_dom - 1)
        def _():
            dom_copy(t, 1).wait_recv()

    def finish_halo_sends(t):
        for o in range(1, n_sub):
            sub_copy(t, subs[o], sub).wait_send()

        @pl.when(dom < n_dom - 1)
        def _():
            dom_copy(t, 0).wait_send()

        @pl.when(dom > 0)
        def _():
            dom_copy(t, 1).wait_send()

    loads[0].wait()
    gather_halo(0)
    loads[1].wait()

    def gather_coarse(d, _):
        for s in range(slots):
            coarse_out[d, s] = coarse[coarse_send[0, s, d]]
        return 0

    lax.fori_loop(0, n, gather_coarse, 0)

    pl.semaphore_wait(barrier, n - 1)
    start_halo(0)

    peers(lambda to, other: coarse_copy(to, other, me).start())

    received[pl.ds(me * slots, slots)] = coarse_out[me]
    pools[0][pl.ds(0, n_fine)] = held[0][...]
    local_pool(0)

    group = math.gcd(n_fine, 4)

    def product(weights, table, index, tiles, into):
        def body(g, _):
            for u in range(group):
                b = g * group + u
                picked = jnp.concatenate([table[index[k, b]] for k in range(tiles)], axis=0)
                into[b] = jnp.dot(
                    weights[b], picked, preferred_element_type=jnp.float32
                ).astype(into.dtype)
            return 0

        lax.fori_loop(0, n_fine // group, body, 0)

    chunk = math.gcd(n_fine, 8)
    live = block_count[0, 0]

    def stored(c):
        at = pl.ds(c * chunk, chunk)
        return pltpu.make_async_copy(out.at[at], out_hbm.at[at], out_sem.at[c])

    for t in range(steps):
        wait_halo(t)
        if t == 0:
            loads[2].wait()
        product(adj, pools[t], adj_index, k_a, summed)
        if t == 0:
            peers(lambda to, other: coarse_copy(to, other, to * n_sub + other).wait_recv())
            for copy in loads[3:]:
                copy.wait()
            product(iw, received, interp_slot, k_i, interp)

        def update(c, _):
            at = pl.ds(c * chunk, chunk)
            h = held[t][at].reshape(chunk * rows, lat)
            joined = jnp.concatenate(
                [
                    h,
                    summed[at].reshape(chunk * rows, lat),
                    interp[at].reshape(chunk * rows, lat),
                ],
                axis=1,
            )
            hidden = jnp.dot(joined, w_in[t], preferred_element_type=jnp.float32)
            hidden = jnp.maximum(hidden + b_in[pl.ds(t, 1)], 0.0).astype(jnp.bfloat16)
            value = jnp.dot(hidden, w_out[t], preferred_element_type=jnp.float32)
            centred = value - jnp.mean(value, axis=-1, keepdims=True)
            variance = jnp.mean(centred * centred, axis=-1, keepdims=True)
            normed = centred * lax.rsqrt(variance + 1e-05) * ln_gain[pl.ds(t, 1)]
            updated = (h.astype(jnp.float32) + normed).reshape(chunk, rows, lat)
            block = c * chunk + lax.broadcasted_iota(jnp.int32, (chunk, rows, lat), 0)
            updated = jnp.where(block < live, updated, 0.0).astype(out.dtype)
            if t == steps - 1:
                out[at] = updated
                stored(c).start()
            else:
                held[t + 1][at] = updated
                pools[t + 1][at] = updated
            return 0

        lax.fori_loop(0, n_fine // chunk, update, 0)
        if t < steps - 1:
            gather_halo(t + 1)
            start_halo(t + 1)
            local_pool(t + 1)

    for t in range(steps):
        finish_halo_sends(t)
    for c in range(n_fine // chunk):
        stored(c).wait()

    peers(lambda to, other: coarse_copy(to, other, me).wait_send())


def per_device(
    n_dom,
    n_sub,
    fine_latent,
    coarse_latent,
    adj_index,
    adj_weight,
    interp_slot,
    interp_weight,
    coarse_send,
    halo_sub_send,
    halo_dom_send,
    block_count,
    w_in,
    b_in,
    w_out,
    ln_gain,
):
    n = n_dom * n_sub
    steps = w_in.shape[0]
    n_fine, rows, lat = fine_latent.shape
    slots = coarse_send.shape[2]
    hs, hd = halo_sub_send.shape[2], halo_dom_send.shape[2]
    pool = n_fine + n_sub * hs + 2 * hd
    kind = fine_latent.dtype

    def vmem(*lead):
        return pltpu.VMEM(lead + (rows, lat), kind)

    dma = pltpu.SemaphoreType.DMA
    scratch = (
        [vmem(n_fine)] * steps
        + [vmem(pool)] * steps
        + [vmem(n_sub, hs)] * steps
        + [vmem(2, hd)] * steps
        + [
            pltpu.VMEM(coarse_latent.shape, kind),
            pltpu.VMEM(adj_weight.shape, kind),
            pltpu.VMEM(interp_weight.shape, kind),
            vmem(n, slots),
            vmem(n * slots),
            vmem(n_fine),
            vmem(n_fine),
            pltpu.VMEM(w_in.shape, w_in.dtype),
            pltpu.VMEM(b_in.shape, b_in.dtype),
            pltpu.VMEM(w_out.shape, w_out.dtype),
            pltpu.VMEM(ln_gain.shape, ln_gain.dtype),
            dma((8,)),
            vmem(n_fine),
            dma((n_fine,)),
            dma((n,)),
            dma((n,)),
            dma((steps, n_sub)),
            dma((steps, n_sub)),
            dma((steps, 2)),
            dma((steps, 2)),
        ]
    )
    smem = pl.BlockSpec(memory_space=pltpu.SMEM)
    hbm = pl.BlockSpec(memory_space=pl.ANY)
    return pl.pallas_call(
        functools.partial(kernel, n_dom, n_sub, steps),
        out_shape=jax.ShapeDtypeStruct(fine_latent.shape, kind),
        in_specs=[smem] * 6 + [hbm] * 8,
        out_specs=hbm,
        scratch_shapes=scratch,
        compiler_params=pltpu.CompilerParams(
            collective_id=0, has_side_effects=True, vmem_limit_bytes=67043328
        ),
        name="graph_steps",
    )(
        adj_index.T,
        interp_slot.T,
        coarse_send.transpose(0, 2, 1),
        halo_sub_send,
        halo_dom_send,
        block_count.reshape(1, 1),
        fine_latent,
        coarse_latent,
        adj_weight,
        interp_weight,
        w_in,
        b_in,
        w_out,
        ln_gain,
    )


def solution(mesh):
    placed = (
        P(("dom", "sub"), None, None),
        P(("dom", "sub"), None, None),
        P(("dom", "sub"), None),
        P(("dom", "sub"), None, None),
        P(("dom", "sub"), None),
        P(("dom", "sub"), None, None),
        P(("dom", "sub"), None, None),
        P(("dom", "sub"), None, None),
        P(("dom", "sub"), None, None),
        P(("dom", "sub")),
        P(),
        P(),
        P(),
        P(),
    )
    return jax.shard_map(
        functools.partial(per_device, mesh.shape["dom"], mesh.shape["sub"]),
        mesh=mesh,
        in_specs=placed,
        out_specs=P(("dom", "sub"), None, None),
        check_vma=False,
    )
```

```python
import functools
import math

import jax
import jax.numpy as jnp
from jax import lax
from jax.experimental import pallas as pl
from jax.experimental.pallas import tpu as pltpu
from jax.sharding import PartitionSpec as P

MESH = pl.DeviceIdType.MESH


def kernel(
    n_dom,
    n_sub,
    steps,
    adj_index,
    interp_slot,
    coarse_send,
    halo_sub_send,
    halo_dom_send,
    block_count,
    fine_hbm,
    coarse_hbm,
    adj_hbm,
    interp_hbm,
    w_in_hbm,
    b_in_hbm,
    w_out_hbm,
    ln_gain_hbm,
    out_hbm,
    *scratch,
):
    held = scratch[:steps]
    pools = scratch[steps : 2 * steps]
    sub_outs = scratch[2 * steps : 3 * steps]
    dom_outs = scratch[3 * steps : 4 * steps]
    (
        coarse,
        adj,
        iw,
        coarse_out,
        received,
        interp,
        summed,
        w_in,
        b_in,
        w_out,
        ln_gain,
        load_sem,
        out,
        out_sem,
        c_send,
        c_recv,
        s_send,
        s_recv,
        d_send,
        d_recv,
    ) = scratch[4 * steps :]

    n = n_dom * n_sub
    dom, sub = lax.axis_index("dom"), lax.axis_index("sub")
    me = dom * n_sub + sub
    n_fine, rows, lat = out_hbm.shape
    slots = coarse_out.shape[1]
    hs = sub_outs[0].shape[1]
    hd = dom_outs[0].shape[1]
    k_a, k_i = adj_index.shape[0], interp_slot.shape[0]

    barrier = pltpu.get_barrier_semaphore()

    def wrapped(position, size):
        return jnp.where(position >= size, position - size, position)

    subs = [wrapped(sub + o, n_sub) for o in range(n_sub)]
    ways = sorted(range(1, n_dom), key=lambda o: abs(o - n_dom // 2))

    def peers(act):
        for o in ways + [0]:
            to = wrapped(dom + o, n_dom)
            for other in subs[1:] if o == 0 else subs:
                act(to, other)

    def greet(to, other):
        pl.semaphore_signal(barrier, inc=1, device_id=(to, other), device_id_type=MESH)

    peers(greet)

    loads = [
        pltpu.make_async_copy(src, dst, load_sem.at[i])
        for i, (src, dst) in enumerate(
            [
                (fine_hbm, held[0]),
                (coarse_hbm, coarse),
                (adj_hbm, adj),
                (interp_hbm, iw),
                (w_in_hbm, w_in),
                (b_in_hbm, b_in),
                (w_out_hbm, w_out),
                (ln_gain_hbm, ln_gain),
            ]
        )
    ]
    for copy in loads:
        copy.start()

    def gather_halo(t):
        for i in range(n_sub):
            for s in range(hs):
                sub_outs[t][i, s] = held[t][halo_sub_send[0, i, s]]
        for i in range(2):
            for s in range(hd):
                dom_outs[t][i, s] = held[t][halo_dom_send[0, i, s]]

    def sub_copy(t, peer, owner):
        return pltpu.make_async_remote_copy(
            src_ref=sub_outs[t].at[peer],
            dst_ref=pools[t].at[pl.ds(n_fine + owner * hs, hs)],
            send_sem=s_send.at[t, peer],
            recv_sem=s_recv.at[t, owner],
            device_id=(dom, peer),
            device_id_type=MESH,
        )

    def dom_copy(t, way):
        target = dom + 1 if way == 0 else dom - 1
        return pltpu.make_async_remote_copy(
            src_ref=dom_outs[t].at[way],
            dst_ref=pools[t].at[pl.ds(n_fine + n_sub * hs + way * hd, hd)],
            send_sem=d_send.at[t, way],
            recv_sem=d_recv.at[t, way],
            device_id=(target, sub),
            device_id_type=MESH,
        )

    def coarse_copy(to, other, owner):
        peer = to * n_sub + other
        return pltpu.make_async_remote_copy(
            src_ref=coarse_out.at[peer],
            dst_ref=received.at[pl.ds(owner * slots, slots)],
            send_sem=c_send.at[peer],
            recv_sem=c_recv.at[owner],
            device_id=(to, other),
            device_id_type=MESH,
        )

    def start_halo(t):
        @pl.when(dom < n_dom - 1)
        def _():
            dom_copy(t, 0).start()

        @pl.when(dom > 0)
        def _():
            dom_copy(t, 1).start()

        for o in range(1, n_sub):
            sub_copy(t, subs[o], sub).start()

    def local_pool(t):
        pools[t][pl.ds(n_fine + sub * hs, hs)] = sub_outs[t][sub]
        base = n_fine + n_sub * hs

        @pl.when(dom == 0)
        def _():
            pools[t][pl.ds(base, hd)] = jnp.zeros((hd, rows, lat), pools[t].dtype)

        @pl.when(dom == n_dom - 1)
        def _():
            pools[t][pl.ds(base + hd, hd)] = jnp.zeros((hd, rows, lat), pools[t].dtype)

    def wait_halo(t):
        for o in range(1, n_sub):
            owner = subs[o]
            sub_copy(t, owner, owner).wait_recv()

        @pl.when(dom > 0)
        def _():
            dom_copy(t, 0).wait_recv()

        @pl.when(dom < n_dom - 1)
        def _():
            dom_copy(t, 1).wait_recv()

    def finish_halo_sends(t):
        for o in range(1, n_sub):
            sub_copy(t, subs[o], sub).wait_send()

        @pl.when(dom < n_dom - 1)
        def _():
            dom_copy(t, 0).wait_send()

        @pl.when(dom > 0)
        def _():
            dom_copy(t, 1).wait_send()

    loads[0].wait()
    gather_halo(0)
    loads[1].wait()

    def gather_coarse(d, _):
        for s in range(slots):
            coarse_out[d, s] = coarse[coarse_send[0, s, d]]
        return 0

    lax.fori_loop(0, n, gather_coarse, 0)

    pl.semaphore_wait(barrier, n - 1)
    start_halo(0)

    peers(lambda to, other: coarse_copy(to, other, me).start())

    received[pl.ds(me * slots, slots)] = coarse_out[me]
    pools[0][pl.ds(0, n_fine)] = held[0][...]
    local_pool(0)

    group = math.gcd(n_fine, 4)

    def product(weights, table, index, tiles, into):
        def body(g, _):
            for u in range(group):
                b = g * group + u
                picked = jnp.concatenate([table[index[k, b]] for k in range(tiles)], axis=0)
                into[b] = jnp.dot(
                    weights[b], picked, preferred_element_type=jnp.float32
                ).astype(into.dtype)
            return 0

        lax.fori_loop(0, n_fine // group, body, 0)

    chunk = math.gcd(n_fine, 8)
    live = block_count[0, 0]

    def stored(c):
        at = pl.ds(c * chunk, chunk)
        return pltpu.make_async_copy(out.at[at], out_hbm.at[at], out_sem.at[c])

    for t in range(steps):
        wait_halo(t)
        if t == 0:
            loads[2].wait()
        product(adj, pools[t], adj_index, k_a, summed)
        if t == 0:
            peers(lambda to, other: coarse_copy(to, other, to * n_sub + other).wait_recv())
            for copy in loads[3:]:
                copy.wait()
            product(iw, received, interp_slot, k_i, interp)

        wide = w_out[t].astype(jnp.float32)
        wide = wide - jnp.mean(wide, axis=-1, keepdims=True)
        high = wide.astype(jnp.bfloat16)
        low = (wide - high.astype(jnp.float32)).astype(jnp.bfloat16)
        split = jnp.concatenate([high, low], axis=1)
        ones = jnp.ones((lat, lat), jnp.bfloat16)

        def update(c, _):
            at = pl.ds(c * chunk, chunk)
            h = held[t][at].reshape(chunk * rows, lat)
            joined = jnp.concatenate(
                [
                    h,
                    summed[at].reshape(chunk * rows, lat),
                    interp[at].reshape(chunk * rows, lat),
                ],
                axis=1,
            )
            hidden = jnp.dot(joined, w_in[t], preferred_element_type=jnp.float32)
            hidden = jnp.maximum(hidden + b_in[pl.ds(t, 1)], 0.0).astype(jnp.bfloat16)
            halves = jnp.dot(hidden, split, preferred_element_type=jnp.float32)
            centred = halves[:, :lat] + halves[:, lat:]
            squares = (centred * centred).astype(jnp.bfloat16)
            variance = jnp.dot(squares, ones, preferred_element_type=jnp.float32) * (1.0 / lat)
            normed = centred * lax.rsqrt(variance + 1e-05) * ln_gain[pl.ds(t, 1)]
            updated = (h.astype(jnp.float32) + normed).reshape(chunk, rows, lat)
            block = c * chunk + lax.broadcasted_iota(jnp.int32, (chunk, rows, lat), 0)
            updated = jnp.where(block < live, updated, 0.0).astype(out.dtype)
            if t == steps - 1:
                out[at] = updated
                stored(c).start()
            else:
                held[t + 1][at] = updated
                pools[t + 1][at] = updated
            return 0

        lax.fori_loop(0, n_fine // chunk, update, 0)
        if t < steps - 1:
            gather_halo(t + 1)
            start_halo(t + 1)
            local_pool(t + 1)

    for t in range(steps):
        finish_halo_sends(t)
    for c in range(n_fine // chunk):
        stored(c).wait()

    peers(lambda to, other: coarse_copy(to, other, me).wait_send())


def per_device(
    n_dom,
    n_sub,
    fine_latent,
    coarse_latent,
    adj_index,
    adj_weight,
    interp_slot,
    interp_weight,
    coarse_send,
    halo_sub_send,
    halo_dom_send,
    block_count,
    w_in,
    b_in,
    w_out,
    ln_gain,
):
    n = n_dom * n_sub
    steps = w_in.shape[0]
    n_fine, rows, lat = fine_latent.shape
    slots = coarse_send.shape[2]
    hs, hd = halo_sub_send.shape[2], halo_dom_send.shape[2]
    pool = n_fine + n_sub * hs + 2 * hd
    kind = fine_latent.dtype

    def vmem(*lead):
        return pltpu.VMEM(lead + (rows, lat), kind)

    dma = pltpu.SemaphoreType.DMA
    scratch = (
        [vmem(n_fine)] * steps
        + [vmem(pool)] * steps
        + [vmem(n_sub, hs)] * steps
        + [vmem(2, hd)] * steps
        + [
            pltpu.VMEM(coarse_latent.shape, kind),
            pltpu.VMEM(adj_weight.shape, kind),
            pltpu.VMEM(interp_weight.shape, kind),
            vmem(n, slots),
            vmem(n * slots),
            vmem(n_fine),
            vmem(n_fine),
            pltpu.VMEM(w_in.shape, w_in.dtype),
            pltpu.VMEM(b_in.shape, b_in.dtype),
            pltpu.VMEM(w_out.shape, w_out.dtype),
            pltpu.VMEM(ln_gain.shape, ln_gain.dtype),
            dma((8,)),
            vmem(n_fine),
            dma((n_fine,)),
            dma((n,)),
            dma((n,)),
            dma((steps, n_sub)),
            dma((steps, n_sub)),
            dma((steps, 2)),
            dma((steps, 2)),
        ]
    )
    smem = pl.BlockSpec(memory_space=pltpu.SMEM)
    hbm = pl.BlockSpec(memory_space=pl.ANY)
    return pl.pallas_call(
        functools.partial(kernel, n_dom, n_sub, steps),
        out_shape=jax.ShapeDtypeStruct(fine_latent.shape, kind),
        in_specs=[smem] * 6 + [hbm] * 8,
        out_specs=hbm,
        scratch_shapes=scratch,
        compiler_params=pltpu.CompilerParams(
            collective_id=0, has_side_effects=True, vmem_limit_bytes=67043328
        ),
        name="graph_steps",
    )(
        adj_index.T,
        interp_slot.T,
        coarse_send.transpose(0, 2, 1),
        halo_sub_send,
        halo_dom_send,
        block_count.reshape(1, 1),
        fine_latent,
        coarse_latent,
        adj_weight,
        interp_weight,
        w_in,
        b_in,
        w_out,
        ln_gain,
    )


def solution(mesh):
    placed = (
        P(("dom", "sub"), None, None),
        P(("dom", "sub"), None, None),
        P(("dom", "sub"), None),
        P(("dom", "sub"), None, None),
        P(("dom", "sub"), None),
        P(("dom", "sub"), None, None),
        P(("dom", "sub"), None, None),
        P(("dom", "sub"), None, None),
        P(("dom", "sub"), None, None),
        P(("dom", "sub")),
        P(),
        P(),
        P(),
        P(),
    )
    return jax.shard_map(
        functools.partial(per_device, mesh.shape["dom"], mesh.shape["sub"]),
        mesh=mesh,
        in_specs=placed,
        out_specs=P(("dom", "sub"), None, None),
        check_vma=False,
    )
```

```python
import functools
import math

import jax
import jax.numpy as jnp
from jax import lax
from jax.experimental import pallas as pl
from jax.experimental.pallas import tpu as pltpu
from jax.sharding import PartitionSpec as P

MESH = pl.DeviceIdType.MESH


def kernel(
    n_dom,
    n_sub,
    steps,
    adj_index,
    interp_slot,
    coarse_send,
    halo_sub_send,
    halo_dom_send,
    block_count,
    fine_hbm,
    coarse_hbm,
    adj_hbm,
    interp_hbm,
    w_in_hbm,
    b_in_hbm,
    w_out_hbm,
    ln_gain_hbm,
    out_hbm,
    *scratch,
):
    held = scratch[:steps]
    pools = scratch[steps : 2 * steps]
    sub_outs = scratch[2 * steps : 3 * steps]
    dom_outs = scratch[3 * steps : 4 * steps]
    (
        coarse,
        adj,
        iw,
        coarse_out,
        received,
        interp,
        summed,
        w_in,
        b_in,
        w_out,
        ln_gain,
        load_sem,
        out,
        out_sem,
        c_send,
        c_recv,
        s_send,
        s_recv,
        d_send,
        d_recv,
    ) = scratch[4 * steps :]

    n = n_dom * n_sub
    dom, sub = lax.axis_index("dom"), lax.axis_index("sub")
    me = dom * n_sub + sub
    n_fine, rows, lat = out_hbm.shape
    slots = coarse_out.shape[1]
    hs = sub_outs[0].shape[1]
    hd = dom_outs[0].shape[1]
    k_a, k_i = adj_index.shape[0], interp_slot.shape[0]

    barrier = pltpu.get_barrier_semaphore()

    def wrapped(position, size):
        return jnp.where(position >= size, position - size, position)

    subs = [wrapped(sub + o, n_sub) for o in range(n_sub)]
    ways = sorted(range(1, n_dom), key=lambda o: abs(o - n_dom // 2))

    def peers(act):
        for o in ways + [0]:
            to = wrapped(dom + o, n_dom)
            for other in subs[1:] if o == 0 else subs:
                act(to, other)

    def greet(to, other):
        pl.semaphore_signal(barrier, inc=1, device_id=(to, other), device_id_type=MESH)

    peers(greet)

    loads = [
        pltpu.make_async_copy(src, dst, load_sem.at[i])
        for i, (src, dst) in enumerate(
            [
                (fine_hbm, held[0]),
                (coarse_hbm, coarse),
                (adj_hbm, adj),
                (interp_hbm, iw),
                (w_in_hbm, w_in),
                (b_in_hbm, b_in),
                (w_out_hbm, w_out),
                (ln_gain_hbm, ln_gain),
            ]
        )
    ]
    for copy in loads:
        copy.start()

    def gather_sub(t):
        for i in range(n_sub):
            for s in range(hs):
                sub_outs[t][i, s] = held[t][halo_sub_send[0, i, s]]

    def gather_dom(t):
        for i in range(2):
            for s in range(hd):
                dom_outs[t][i, s] = held[t][halo_dom_send[0, i, s]]

    def sub_copy(t, peer, owner):
        return pltpu.make_async_remote_copy(
            src_ref=sub_outs[t].at[peer],
            dst_ref=pools[t].at[pl.ds(n_fine + owner * hs, hs)],
            send_sem=s_send.at[t, peer],
            recv_sem=s_recv.at[t, owner],
            device_id=(dom, peer),
            device_id_type=MESH,
        )

    def dom_copy(t, way):
        target = dom + 1 if way == 0 else dom - 1
        return pltpu.make_async_remote_copy(
            src_ref=dom_outs[t].at[way],
            dst_ref=pools[t].at[pl.ds(n_fine + n_sub * hs + way * hd, hd)],
            send_sem=d_send.at[t, way],
            recv_sem=d_recv.at[t, way],
            device_id=(target, sub),
            device_id_type=MESH,
        )

    def coarse_copy(to, other, owner):
        peer = to * n_sub + other
        return pltpu.make_async_remote_copy(
            src_ref=coarse_out.at[peer],
            dst_ref=received.at[pl.ds(owner * slots, slots)],
            send_sem=c_send.at[peer],
            recv_sem=c_recv.at[owner],
            device_id=(to, other),
            device_id_type=MESH,
        )

    def start_dom(t):
        @pl.when(dom < n_dom - 1)
        def _():
            dom_copy(t, 0).start()

        @pl.when(dom > 0)
        def _():
            dom_copy(t, 1).start()

    def start_sub(t):
        for o in range(1, n_sub):
            sub_copy(t, subs[o], sub).start()

    def local_pool(t):
        pools[t][pl.ds(n_fine + sub * hs, hs)] = sub_outs[t][sub]
        base = n_fine + n_sub * hs

        @pl.when(dom == 0)
        def _():
            pools[t][pl.ds(base, hd)] = jnp.zeros((hd, rows, lat), pools[t].dtype)

        @pl.when(dom == n_dom - 1)
        def _():
            pools[t][pl.ds(base + hd, hd)] = jnp.zeros((hd, rows, lat), pools[t].dtype)

    def wait_halo(t):
        for o in range(1, n_sub):
            owner = subs[o]
            sub_copy(t, owner, owner).wait_recv()

        @pl.when(dom > 0)
        def _():
            dom_copy(t, 0).wait_recv()

        @pl.when(dom < n_dom - 1)
        def _():
            dom_copy(t, 1).wait_recv()

    def finish_halo_sends(t):
        for o in range(1, n_sub):
            sub_copy(t, subs[o], sub).wait_send()

        @pl.when(dom < n_dom - 1)
        def _():
            dom_copy(t, 0).wait_send()

        @pl.when(dom > 0)
        def _():
            dom_copy(t, 1).wait_send()

    loads[0].wait()
    gather_dom(0)
    gather_sub(0)
    loads[1].wait()

    def gather_coarse(d, _):
        for s in range(slots):
            coarse_out[d, s] = coarse[coarse_send[0, s, d]]
        return 0

    lax.fori_loop(0, n, gather_coarse, 0)

    pl.semaphore_wait(barrier, n - 1)
    start_dom(0)
    start_sub(0)

    peers(lambda to, other: coarse_copy(to, other, me).start())

    received[pl.ds(me * slots, slots)] = coarse_out[me]
    pools[0][pl.ds(0, n_fine)] = held[0][...]
    local_pool(0)

    group = math.gcd(n_fine, 16)

    def product(weights, table, index, tiles, into):
        def body(g, _):
            for u in range(group):
                b = g * group + u
                picked = jnp.concatenate([table[index[k, b]] for k in range(tiles)], axis=0)
                into[b] = jnp.dot(
                    weights[b], picked, preferred_element_type=jnp.float32
                ).astype(into.dtype)
            return 0

        lax.fori_loop(0, n_fine // group, body, 0)

    chunk = math.gcd(n_fine, 32)
    live = block_count[0, 0]

    def stored(c):
        at = pl.ds(c * chunk, chunk)
        return pltpu.make_async_copy(out.at[at], out_hbm.at[at], out_sem.at[c])

    for t in range(steps):
        wait_halo(t)
        if t == 0:
            loads[2].wait()
        product(adj, pools[t], adj_index, k_a, summed)
        if t == 0:
            peers(lambda to, other: coarse_copy(to, other, to * n_sub + other).wait_recv())
            for copy in loads[3:]:
                copy.wait()
            product(iw, received, interp_slot, k_i, interp)

        wide = w_out[t].astype(jnp.float32)
        wide = wide - jnp.mean(wide, axis=-1, keepdims=True)
        high = wide.astype(jnp.bfloat16)
        low = (wide - high.astype(jnp.float32)).astype(jnp.bfloat16)
        split = jnp.concatenate([high, low], axis=1)
        ones = jnp.ones((lat, lat), jnp.bfloat16)

        def update(c, _):
            at = pl.ds(c * chunk, chunk)
            h = held[t][at].reshape(chunk * rows, lat)
            joined = jnp.concatenate(
                [
                    h,
                    summed[at].reshape(chunk * rows, lat),
                    interp[at].reshape(chunk * rows, lat),
                ],
                axis=1,
            )
            hidden = jnp.dot(joined, w_in[t], preferred_element_type=jnp.float32)
            hidden = jnp.maximum(hidden + b_in[pl.ds(t, 1)], 0.0).astype(jnp.bfloat16)
            halves = jnp.dot(hidden, split, preferred_element_type=jnp.float32)
            centred = halves[:, :lat] + halves[:, lat:]
            squares = (centred * centred).astype(jnp.bfloat16)
            variance = jnp.dot(squares, ones, preferred_element_type=jnp.float32) * (1.0 / lat)
            normed = centred * lax.rsqrt(variance + 1e-05) * ln_gain[pl.ds(t, 1)]
            updated = (h.astype(jnp.float32) + normed).reshape(chunk, rows, lat)
            block = c * chunk + lax.broadcasted_iota(jnp.int32, (chunk, rows, lat), 0)
            updated = jnp.where(block < live, updated, 0.0).astype(out.dtype)
            if t == steps - 1:
                out[at] = updated
                stored(c).start()
            else:
                held[t + 1][at] = updated
                pools[t + 1][at] = updated
            return 0

        lax.fori_loop(0, n_fine // chunk, update, 0)
        if t < steps - 1:
            gather_dom(t + 1)
            start_dom(t + 1)
            gather_sub(t + 1)
            start_sub(t + 1)
            local_pool(t + 1)

    for t in range(steps):
        finish_halo_sends(t)
    for c in range(n_fine // chunk):
        stored(c).wait()

    peers(lambda to, other: coarse_copy(to, other, me).wait_send())


def per_device(
    n_dom,
    n_sub,
    fine_latent,
    coarse_latent,
    adj_index,
    adj_weight,
    interp_slot,
    interp_weight,
    coarse_send,
    halo_sub_send,
    halo_dom_send,
    block_count,
    w_in,
    b_in,
    w_out,
    ln_gain,
):
    n = n_dom * n_sub
    steps = w_in.shape[0]
    n_fine, rows, lat = fine_latent.shape
    slots = coarse_send.shape[2]
    hs, hd = halo_sub_send.shape[2], halo_dom_send.shape[2]
    pool = n_fine + n_sub * hs + 2 * hd
    kind = fine_latent.dtype

    def vmem(*lead):
        return pltpu.VMEM(lead + (rows, lat), kind)

    dma = pltpu.SemaphoreType.DMA
    scratch = (
        [vmem(n_fine)] * steps
        + [vmem(pool)] * steps
        + [vmem(n_sub, hs)] * steps
        + [vmem(2, hd)] * steps
        + [
            pltpu.VMEM(coarse_latent.shape, kind),
            pltpu.VMEM(adj_weight.shape, kind),
            pltpu.VMEM(interp_weight.shape, kind),
            vmem(n, slots),
            vmem(n * slots),
            vmem(n_fine),
            vmem(n_fine),
            pltpu.VMEM(w_in.shape, w_in.dtype),
            pltpu.VMEM(b_in.shape, b_in.dtype),
            pltpu.VMEM(w_out.shape, w_out.dtype),
            pltpu.VMEM(ln_gain.shape, ln_gain.dtype),
            dma((8,)),
            vmem(n_fine),
            dma((n_fine,)),
            dma((n,)),
            dma((n,)),
            dma((steps, n_sub)),
            dma((steps, n_sub)),
            dma((steps, 2)),
            dma((steps, 2)),
        ]
    )
    smem = pl.BlockSpec(memory_space=pltpu.SMEM)
    hbm = pl.BlockSpec(memory_space=pl.ANY)
    return pl.pallas_call(
        functools.partial(kernel, n_dom, n_sub, steps),
        out_shape=jax.ShapeDtypeStruct(fine_latent.shape, kind),
        in_specs=[smem] * 6 + [hbm] * 8,
        out_specs=hbm,
        scratch_shapes=scratch,
        compiler_params=pltpu.CompilerParams(
            collective_id=0, has_side_effects=True, vmem_limit_bytes=67043328
        ),
        name="graph_steps",
    )(
        adj_index.T,
        interp_slot.T,
        coarse_send.transpose(0, 2, 1),
        halo_sub_send,
        halo_dom_send,
        block_count.reshape(1, 1),
        fine_latent,
        coarse_latent,
        adj_weight,
        interp_weight,
        w_in,
        b_in,
        w_out,
        ln_gain,
    )


def solution(mesh):
    placed = (
        P(("dom", "sub"), None, None),
        P(("dom", "sub"), None, None),
        P(("dom", "sub"), None),
        P(("dom", "sub"), None, None),
        P(("dom", "sub"), None),
        P(("dom", "sub"), None, None),
        P(("dom", "sub"), None, None),
        P(("dom", "sub"), None, None),
        P(("dom", "sub"), None, None),
        P(("dom", "sub")),
        P(),
        P(),
        P(),
        P(),
    )
    return jax.shard_map(
        functools.partial(per_device, mesh.shape["dom"], mesh.shape["sub"]),
        mesh=mesh,
        in_specs=placed,
        out_specs=P(("dom", "sub"), None, None),
        check_vma=False,
    )
```
